32 devices in a mesh: groups: 2 (over y), expo: 4 (over z), tile: 4 (over x, core).
Axes of the slice: x: 2, y: 2, z: 4, core: 2. Of those that a mesh axis runs over, the one named last changes fastest.
Arguments:
- template: bfloat16 [8, 64, 4096], P(('groups', 'expo'), 'tile'), parts along dimension 0
- science: bfloat16 [8, 1, 64, 4096], P(('groups', 'expo'), None, 'tile'), parts along dimension 0
- plan: int32 [8], P('groups'), parts along dimension 0, may hold values from 0 to 3, as said below
- orders: int32 [6, 2], replicated, may hold values from 0 to 2
- coadd_weight: float32 [8, 1], P(('groups', 'expo')), parts along dimension 0, may hold values from 0.3 to 3
- intersection: int32 [8, 1], P(('groups', 'expo')), parts along dimension 0, may hold values 0 or 1
Outputs:
- coadd: float32 [2, 64, 4096], P('groups', 'tile', 'expo'), parts along dimension 0
- coeffs: float32 [8, 1, 13], P(('groups', 'expo')), parts along dimension 0
The draws below stay inside these ranges and needn't reach their ends.
There are 2 independent parts, one for each index of `groups`. The reference program is written for one: setup_inputs(seed, part) draws one part's arguments, and reference() takes and returns one part's arrays. A program takes and returns all parts, laid end to end along the dimension named above; an argument that names none is the same for every part. Nothing has to cross between parts.
Inputs may be any that keep to these rules, and one draw needn't show every extreme that they name: `plan`: a permutation of the group's patch indices.
All inputs are finite; a program needn't handle non-finite values. No bound on the sum of `intersection` on one device may be relied on, other than what follows from the above.
Results may differ from the reference program's by a relative error of at most 0.0061.
Values may be sent and summed in bfloat16 or wider, within the bound.
A program may use at most 64 MiB of HBM per device.

```python
import math
import jax
import jax.numpy as jnp
from jax import lax

W = 4096
HALF = 15
NB = 6
NU = 13
ROWS = 64
EXPOS = 4
PATCHES = 4
STEPS = 1


def template_field(key):
    field = jax.random.normal(jax.random.fold_in(key, 11), (PATCHES, ROWS, W), jnp.float32)
    return jnp.clip(field, -6.0, 6.0)


def plan_ids(key):
    order_ids = jax.random.permutation(jax.random.fold_in(key, 41), PATCHES)
    return order_ids.astype(jnp.int32)


def draw_template(key, part):
    return template_field(key).astype(jnp.bfloat16)


def draw_plan(key, part):
    return plan_ids(key)


def draw_science(key, part):
    field = template_field(key)
    picked = field[plan_ids(key)[:STEPS]]
    gains = jnp.exp(jax.random.uniform(jax.random.fold_in(key, 13), (EXPOS, STEPS), jnp.float32, -0.7, 0.7))
    shifts = jax.random.randint(jax.random.fold_in(key, 14), (EXPOS, STEPS, 2), -1, 2)
    noise = 0.5 * jax.random.normal(jax.random.fold_in(key, 15), (EXPOS, STEPS, ROWS, W), jnp.float32)

    def one_image(image, shift_pair):
        moved = jnp.roll(image, shift_pair[0], axis=0)
        return jnp.roll(moved, shift_pair[1], axis=1)
    moved_all = jax.vmap(jax.vmap(one_image, in_axes=(0, 0)), in_axes=(None, 0))(picked, shifts)
    return (gains[:, :, None, None] * moved_all + noise).astype(jnp.bfloat16)


def touch_ends(drawn, stream_key, least, high):
    longest = drawn.shape.index(max(drawn.shape))
    spots = []
    for shift in (0, 1):
        where = [jax.random.randint(jax.random.fold_in(stream_key, axis), (), 0, length) for axis, length in enumerate(drawn.shape)]
        where[longest] = (where[longest] + shift) % drawn.shape[longest]
        spots.append(tuple(where))
    return drawn.at[spots[0]].set(least).at[spots[1]].set(high)


def levels(stream_key, dims, split, smallest, largest):
    level, own = 1.0, jax.random.fold_in(stream_key, 6)
    for axis_at, blocks in split:
        draws = jnp.exp(jax.random.uniform(jax.random.fold_in(own, axis_at), (blocks,), jnp.float32, smallest / len(split), largest / len(split)))
        level = level * jnp.repeat(draws, dims[axis_at] // blocks).reshape([-1 if axis == axis_at else 1 for axis in range(len(dims))])
    return level


def setup_inputs(seed: int = 0, part: int = 0) -> dict:
    keys = jax.random.split(jax.random.key(seed), 7)
    part_keys = jax.random.split(jax.random.fold_in(keys[6], part), 7)
    return {
        "template": draw_template(jax.random.fold_in(jax.random.fold_in(keys[6], part), 71), part),
        "science": draw_science(jax.random.fold_in(jax.random.fold_in(keys[6], part), 71), part),
        "plan": draw_plan(jax.random.fold_in(jax.random.fold_in(keys[6], part), 71), part),
        "orders": touch_ends(jax.random.randint(keys[3], (NB, 2), 0, 3), jax.random.fold_in(keys[3], 1), 0, 2).astype(jnp.int32),
        "coadd_weight": jnp.clip(jnp.exp(math.log(3.0) - 2.3025851 * jax.random.uniform(part_keys[4], (EXPOS, STEPS), jnp.float32) ** levels(part_keys[4], (EXPOS, STEPS), ((0, 4),), -0.2, 0.2)), 0.3, 3.0),
        "intersection": touch_ends((jax.random.randint(part_keys[5], (EXPOS, STEPS), 0, 4) < 3).astype(jnp.int32), jax.random.fold_in(part_keys[5], 1), 0, 1),
    }


SIGMAS = (0.8, 1.4, 2.2, 3.0, 4.0, 5.5)
RIDGE = 0.05

def make_filters(orders):
    taps_pos = jnp.arange(2 * HALF + 1).astype(jnp.float32) - HALF
    row_list = []
    col_list = []
    for basis in range(NB):
        sigma = SIGMAS[basis]
        envelope = jnp.exp(-taps_pos * taps_pos / (2.0 * sigma * sigma))

        def power(order):
            return jnp.where(order == 0, 1.0, jnp.where(order == 1, taps_pos, taps_pos * taps_pos))
        row_filter = envelope * power(orders[basis, 0])
        col_filter = envelope * power(orders[basis, 1])
        row_list.append(row_filter / jnp.sqrt(jnp.sum(row_filter * row_filter)))
        col_list.append(col_filter / jnp.sqrt(jnp.sum(col_filter * col_filter)))
    return (jnp.stack(row_list).astype(jnp.bfloat16), jnp.stack(col_list).astype(jnp.bfloat16))

def convolve(patch, row_filters, col_filters):
    padded = jnp.pad(patch, ((HALF, HALF), (0, 0))).astype(jnp.float32)
    row_taps = row_filters.astype(jnp.float32)
    col_taps = col_filters.astype(jnp.float32)
    rowconv = jnp.zeros((NB, ROWS, W), jnp.float32)
    for tap in range(2 * HALF + 1):
        rowconv = rowconv + row_taps[:, tap][:, None, None] * padded[None, tap:tap + ROWS, :]
    rowconv = rowconv.astype(jnp.bfloat16)
    padded_cols = jnp.pad(rowconv, ((0, 0), (0, 0), (HALF, HALF))).astype(jnp.float32)
    conv = jnp.zeros((NB, ROWS, W), jnp.float32)
    for tap in range(2 * HALF + 1):
        conv = conv + col_taps[:, tap][:, None, None] * padded_cols[:, :, tap:tap + W]
    return conv

def reference(template, science, plan, orders, coadd_weight, intersection):
    row_filters, col_filters = make_filters(orders)
    column_pos = 2.0 * (jnp.arange(W).astype(jnp.float32) + 0.5) / W - 1.0
    coadds = []
    fitted = []
    for step in range(STEPS):
        patch = template[plan[step]]
        conv = convolve(patch, row_filters, col_filters)
        fields = jnp.concatenate([conv, conv * column_pos, jnp.ones((1, ROWS, W), jnp.float32)], axis=0)
        fields = fields.reshape(NU, ROWS * W)
        normal_matrix = jnp.dot(fields, fields.T, precision=lax.Precision.HIGHEST)
        normal_matrix = normal_matrix + RIDGE * (jnp.trace(normal_matrix) / NU) * jnp.eye(NU, dtype=jnp.float32)
        exposure_image = science[:, step].astype(jnp.float32).reshape(EXPOS, ROWS * W)
        projections = jnp.dot(exposure_image, fields.T, precision=lax.Precision.HIGHEST)
        factor = jnp.linalg.cholesky(normal_matrix)
        coeffs = jax.scipy.linalg.cho_solve((factor, True), projections.T).T
        model = jnp.dot(coeffs, fields, precision=lax.Precision.HIGHEST)
        difference = exposure_image - model
        weights = coadd_weight[:, step] * intersection[:, step].astype(jnp.float32)
        coadds.append(jnp.dot(weights, difference, precision=lax.Precision.HIGHEST).reshape(ROWS, W))
        fitted.append(coeffs)
    return (jnp.stack(coadds), jnp.stack(fitted, axis=1))
```

```python
import functools

import jax
import jax.numpy as jnp
from jax import lax
from jax.experimental import pallas as pl
from jax.experimental.pallas import tpu as pltpu
from jax.sharding import PartitionSpec as P

HALF = 15
NB = 6
NU = 13


SIGMAS = (0.8, 1.4, 2.2, 3.0, 4.0, 5.5)
RIDGE = 0.05


def broadcast(block, axis, holder):
    block = jnp.where(lax.axis_index(axis) == holder, block, jnp.zeros_like(block))
    return lax.psum(block, axis)


def extended(x, sides, width):
    for axis, dim in sides:
        size, length = (lax.axis_size(axis), x.shape[dim])
        up = [(i, (i + 1) % size) for i in range(size - 1)]
        down = [(j, i) for i, j in up]
        last = lax.slice_in_dim(x, length - width, length, axis=dim)
        first = lax.slice_in_dim(x, 0, width, axis=dim)
        before = lax.ppermute(last, axis, up)
        after = lax.ppermute(first, axis, down)
        x = jnp.concatenate([before, x, after], axis=dim)
    return x


def make_filters(orders):
    taps_pos = jnp.arange(2 * HALF + 1).astype(jnp.float32) - HALF
    row_list = []
    col_list = []
    for basis in range(NB):
        sigma = SIGMAS[basis]
        envelope = jnp.exp(-taps_pos * taps_pos / (2.0 * sigma * sigma))

        def power(order):
            return jnp.where(order == 0, 1.0, jnp.where(order == 1, taps_pos, taps_pos * taps_pos))

        row_filter = envelope * power(orders[basis, 0])
        col_filter = envelope * power(orders[basis, 1])
        row_list.append(row_filter / jnp.sqrt(jnp.sum(row_filter * row_filter)))
        col_list.append(col_filter / jnp.sqrt(jnp.sum(col_filter * col_filter)))
    return (jnp.stack(row_list).astype(jnp.bfloat16), jnp.stack(col_list).astype(jnp.bfloat16))


def band_matrix(filters, out_len, in_len):
    offset = jnp.arange(in_len)[None, :] - jnp.arange(out_len)[:, None]
    taps_idx = jnp.arange(2 * HALF + 1)
    picks = (offset[:, :, None] == taps_idx[None, None, :]).astype(jnp.float32)
    band = jnp.einsum("ijt,kt->kij", picks, filters.astype(jnp.float32))
    return band.astype(jnp.bfloat16)


def per_device(template, science, plan, orders, coadd_weight, intersection):
    row_filters, col_filters = make_filters(orders)
    rows = template.shape[1]
    width = template.shape[2]
    blocks_count = width // 128
    steps_count = science.shape[1]
    row_band = band_matrix(row_filters, rows, rows + 2 * HALF)
    col_band = jnp.transpose(band_matrix(col_filters, 128, 128 + 2 * HALF), (0, 2, 1))
    column_pos = 2.0 * (jnp.arange(width).astype(jnp.float32) + 0.5) / width - 1.0
    pieces = []
    fitted = []
    for step in range(steps_count):
        owner_index = plan[step]
        received = broadcast(template[0], "expo", owner_index)
        padded = extended(received, (("tile", 0),), HALF)
        rowconv = jnp.einsum(
            "kij,jw->kiw", row_band, padded, preferred_element_type=jnp.float32
        ).astype(jnp.bfloat16)
        blocks = rowconv.reshape(NB, rows, blocks_count, 128)
        empty_rim = jnp.zeros((NB, rows, 1, HALF), jnp.bfloat16)
        previous = jnp.concatenate([empty_rim, blocks[:, :, :-1, 128 - HALF :]], axis=2)
        following = jnp.concatenate([blocks[:, :, 1:, :HALF], empty_rim], axis=2)
        window = jnp.concatenate([previous, blocks, following], axis=3)
        conv = jnp.einsum("krbj,kjc->krbc", window, col_band, preferred_element_type=jnp.float32)
        conv = conv.reshape(NB, rows, width)
        fields = jnp.concatenate(
            [conv, conv * column_pos, jnp.ones((1, rows, width), jnp.float32)], axis=0
        )
        fields = fields.reshape(NU, rows * width)
        exposure_image = science[0, step].astype(jnp.float32).reshape(rows * width)
        normal_local = jnp.dot(fields, fields.T, precision=lax.Precision.HIGHEST)
        project_local = jnp.dot(fields, exposure_image, precision=lax.Precision.HIGHEST)
        normal_matrix, projections = lax.psum((normal_local, project_local), "tile")
        normal_matrix = normal_matrix + RIDGE * (jnp.trace(normal_matrix) / NU) * jnp.eye(
            NU, dtype=jnp.float32
        )
        factor = jnp.linalg.cholesky(normal_matrix)
        coeffs = jax.scipy.linalg.cho_solve((factor, True), projections)
        model = jnp.dot(coeffs, fields, precision=lax.Precision.HIGHEST)
        difference = exposure_image - model
        weight_now = coadd_weight[0, step] * intersection[0, step].astype(jnp.float32)
        pieces.append((weight_now * difference).reshape(rows, width))
        fitted.append(coeffs)
    weighted = jnp.stack(pieces)
    received_parts = lax.all_to_all(weighted[None], "expo", split_axis=3, concat_axis=0, tiled=True)
    coadd = jnp.sum(received_parts, axis=0)
    return (coadd, jnp.stack(fitted)[None])


LANES = 128
WIDE = 256
PAIRS = [(u, v) for u in range(NB) for v in range(u + 1)]
MESH = pl.DeviceIdType.MESH


def taps(position, sigma, order):
    power = jnp.where(order == 0, 1.0, jnp.where(order == 1, position, position * position))
    value = jnp.exp(-position * position / (2.0 * sigma * sigma)) * power
    return jnp.where(jnp.abs(position) <= HALF, value, 0.0)


def fused(
    dims,
    template_ref,
    science_ref,
    plan_ref,
    orders_ref,
    weight_ref,
    inter_ref,
    coadd_ref,
    coeffs_ref,
    tbuf,
    sbuf,
    rbuf,
    row_band,
    col_band,
    conv_ref,
    stat_ref,
    local_sem,
    tsend,
    trecv,
    ssend,
    srecv,
    fsend,
    frecv,
    rsend,
    rrecv,
):
    expos, tiles, rows, width, cols = dims
    per = cols // LANES
    span = cols + 2 * LANES
    blocks = cols // WIDE
    chunks = [(b, h) for b in range(blocks) for h in range(WIDE // LANES)]
    me = lax.axis_index("expo")
    tile = lax.axis_index("tile")

    def others():
        for de in range(expos):
            for dt in range(tiles):
                if de or dt:
                    yield de * tiles + dt, (me + de) % expos, (tile + dt) % tiles

    barrier = pltpu.get_barrier_semaphore()
    for _, e, t in others():
        pl.semaphore_signal(
            barrier, inc=1, device_id={"expo": e, "tile": t}, device_id_type=MESH
        )

    def source_start(e):
        return e * per - 1 + (expos - 1 - e) // (expos - 1) - e // (expos - 1)

    def source_columns(e):
        return pl.ds(pl.multiple_of(source_start(e) * LANES, LANES), span)

    def window_columns(e):
        return pl.ds(pl.multiple_of((source_start(e) - e * per + 2) * LANES, LANES), span)

    def own_columns(e):
        return pl.ds(pl.multiple_of(e * cols, LANES), cols)

    mine = pltpu.make_async_copy(
        template_ref.at[0, :, source_columns(me)],
        tbuf.at[me, 1, :, window_columns(me)],
        local_sem.at[0],
    )
    mine.start()
    mine_science = pltpu.make_async_copy(
        science_ref.at[0, 0, :, own_columns(me)], sbuf.at[me], local_sem.at[1]
    )
    mine_science.start()
    pl.semaphore_wait(barrier, expos * tiles - 1)

    def template_copy(d, target, holder):
        return pltpu.make_async_remote_copy(
            src_ref=template_ref.at[0, :, source_columns(target)],
            dst_ref=tbuf.at[holder, 1, :, window_columns(target)],
            send_sem=tsend.at[d],
            recv_sem=trecv.at[d],
            device_id={"expo": target},
            device_id_type=MESH,
        )

    def science_copy(d, target, holder):
        return pltpu.make_async_remote_copy(
            src_ref=science_ref.at[0, 0, :, own_columns(target)],
            dst_ref=sbuf.at[holder],
            send_sem=ssend.at[d],
            recv_sem=srecv.at[d],
            device_id={"expo": target},
            device_id_type=MESH,
        )

    def forward_copy(d, holder, side):
        target = tile + 1 if side == 0 else tile - 1
        return pltpu.make_async_remote_copy(
            src_ref=tbuf.at[holder, 1, :, window_columns(me)],
            dst_ref=tbuf.at[holder, 2 * side, :, window_columns(me)],
            send_sem=fsend.at[side, d],
            recv_sem=frecv.at[side, d],
            device_id={"tile": target},
            device_id_type=MESH,
        )

    def forward(d, holder):
        @pl.when(tile < tiles - 1)
        def _():
            forward_copy(d, holder, 0).start()

        @pl.when(tile > 0)
        def _():
            forward_copy(d, holder, 1).start()

    for d in range(1, expos):
        template_copy(d, (me + d) % expos, me).start()
    mine.wait()
    forward(0, me)
    for d in range(1, expos):
        science_copy(d, (me + d) % expos, me).start()

    position = lax.broadcasted_iota(jnp.int32, (1, LANES), 1).astype(jnp.float32) - HALF
    for k in range(NB):
        sigma = SIGMAS[k]
        for side, length in ((0, rows), (1, LANES)):
            order = jnp.full((1, LANES), orders_ref[k, side], jnp.int32)
            line = taps(position, sigma, order)
            root = jnp.sqrt(jnp.sum(line * line, axis=1, keepdims=True))
            scale = 1.0 / root
            if side == 0:
                shape = (rows, 3 * rows)
                offset = (
                    lax.broadcasted_iota(jnp.int32, shape, 1)
                    - lax.broadcasted_iota(jnp.int32, shape, 0)
                    - rows
                ).astype(jnp.float32)
                band = taps(offset, sigma, jnp.full(shape, orders_ref[k, side], jnp.int32))
                row_band[k * rows : (k + 1) * rows, :] = (band * scale).astype(jnp.bfloat16)
            else:
                shape = (LANES, LANES)
                delta = lax.broadcasted_iota(jnp.int32, shape, 0) - lax.broadcasted_iota(
                    jnp.int32, shape, 1
                )
                column_order = jnp.full(shape, orders_ref[k, side], jnp.int32)
                zero = jnp.zeros(shape, jnp.bfloat16)
                parts = {}
                for kind in range(3):
                    offset = (delta + (kind - 1) * LANES).astype(jnp.float32)
                    band = taps(offset, sigma, column_order)
                    parts[kind] = (band * scale).astype(jnp.bfloat16)
                for jb in range(WIDE // LANES + 2):
                    for cb in range(WIDE // LANES):
                        col_band[
                            k,
                            jb * LANES : (jb + 1) * LANES,
                            cb * LANES : (cb + 1) * LANES,
                        ] = parts.get(jb - cb, zero)

    for d in range(1, expos):
        holder = (me + expos - d) % expos
        template_copy(d, me, holder).wait_recv()
        forward(d, holder)

    @pl.when(tile > 0)
    def _():
        for d in range(expos):
            forward_copy(d, (me + expos - d) % expos, 0).wait_recv()

    @pl.when(tile < tiles - 1)
    def _():
        for d in range(expos):
            forward_copy(d, (me + expos - d) % expos, 1).wait_recv()

    @pl.when(tile < tiles - 1)
    def _():
        for d in range(expos):
            forward_copy(d, (me + expos - d) % expos, 0).wait_send()

    @pl.when(tile > 0)
    def _():
        for d in range(expos):
            forward_copy(d, (me + expos - d) % expos, 1).wait_send()

    owner = plan_ref[0]
    shape = (rows, span)
    column = lax.broadcasted_iota(jnp.int32, shape, 1) + (me * cols - LANES)
    inside = (column >= 0) & (column < width)
    pieces = []
    for part in range(3):
        block = tbuf[owner, part, :, LANES : LANES + span].astype(jnp.float32)
        keep = inside
        if part == 0:
            keep = keep & (jnp.full(shape, tile, jnp.int32) > 0)
        if part == 2:
            keep = keep & (jnp.full(shape, tile, jnp.int32) < tiles - 1)
        pieces.append(jnp.where(keep, block, 0.0).astype(jnp.bfloat16))
    rows_window = jnp.concatenate(pieces, axis=0)
    rowconv = jnp.dot(
        row_band[...], rows_window, preferred_element_type=jnp.float32
    ).astype(jnp.bfloat16)
    for k in range(NB):
        mine_rows = rowconv[k * rows : (k + 1) * rows]
        windows = jnp.concatenate(
            [mine_rows[:, b * WIDE : (b + 1) * WIDE + 2 * LANES] for b in range(blocks)], axis=0
        )
        conv_ref[k] = jnp.dot(windows, col_band[k], preferred_element_type=jnp.float32)

    def conv_at(k, b, h):
        return conv_ref[k, b * rows : (b + 1) * rows, h * LANES : (h + 1) * LANES]

    def science_at(e, b, h):
        start = b * WIDE + h * LANES
        return sbuf[e, :, start : start + LANES].astype(jnp.float32)

    def fold(x):
        return x.reshape(rows // 8, 8, LANES).sum(axis=0)

    lane = lax.broadcasted_iota(jnp.int32, (1, LANES), 1)
    columns = {}
    for b, h in chunks:
        place = (me * cols + b * WIDE + h * LANES + lane).astype(jnp.float32)
        columns[b, h] = 2.0 * (place + 0.5) / width - 1.0

    def put(index, value):
        stat_ref[index : index + 1, :] = jnp.sum(value, axis=0, keepdims=True)

    count = 3 * len(PAIRS) + 2 * NB
    for index, (u, v) in enumerate(PAIRS):
        sums = [0.0, 0.0, 0.0]
        for b, h in chunks:
            product = fold(conv_at(u, b, h) * conv_at(v, b, h))
            once = product * columns[b, h]
            sums = [sums[0] + product, sums[1] + once, sums[2] + once * columns[b, h]]
        for moment in range(3):
            put(3 * index + moment, sums[moment])
    for u in range(NB):
        sums = [0.0, 0.0]
        for b, h in chunks:
            product = fold(conv_at(u, b, h))
            sums = [sums[0] + product, sums[1] + product * columns[b, h]]
        for moment in range(2):
            put(3 * len(PAIRS) + NB * moment + u, sums[moment])

    mine_science.wait()
    for d in range(1, expos):
        science_copy(d, me, (me + expos - d) % expos).wait_recv()
    for e in range(expos):
        for u in range(NB):
            sums = [0.0, 0.0]
            for b, h in chunks:
                product = fold(conv_at(u, b, h) * science_at(e, b, h))
                sums = [sums[0] + product, sums[1] + product * columns[b, h]]
            for moment in range(2):
                put(count + (NB * moment + u) * expos + e, sums[moment])
        total = 0.0
        for b, h in chunks:
            total = total + fold(science_at(e, b, h))
        put(count + 2 * NB * expos + e, total)
    used = count + NU * expos
    if used < LANES:
        stat_ref[used:LANES, :] = jnp.zeros((LANES - used, LANES), jnp.float32)

    reduced = jnp.sum(jnp.transpose(stat_ref[...]), axis=0, keepdims=True)
    weight = weight_ref[0, 0] * inter_ref[0, 0].astype(jnp.float32)
    rbuf[me, tile, :, :LANES] = reduced
    rbuf[me, tile, :, LANES:] = jnp.full((1, LANES), weight, jnp.float32)

    def stat_copy(index, e, t, to_e, to_t):
        return pltpu.make_async_remote_copy(
            src_ref=rbuf.at[e, t],
            dst_ref=rbuf.at[e, t],
            send_sem=rsend.at[index],
            recv_sem=rrecv.at[index],
            device_id={"expo": to_e, "tile": to_t},
            device_id_type=MESH,
        )

    for index, e, t in others():
        stat_copy(index, me, tile, e, t).start()
    for d in range(1, expos):
        template_copy(d, (me + d) % expos, me).wait_send()
        science_copy(d, (me + d) % expos, me).wait_send()
    for de in range(expos):
        for dt in range(tiles):
            if de or dt:
                e = (me + expos - de) % expos
                t = (tile + tiles - dt) % tiles
                stat_copy(de * tiles + dt, e, t, e, t).wait_recv()

    total = rbuf[0, 0, :, :LANES]
    for e in range(expos):
        for t in range(tiles):
            if e or t:
                total = total + rbuf[e, t, :, :LANES]
    stat_ref[...] = jnp.transpose(jnp.broadcast_to(total, (LANES, LANES)))

    def value(index):
        return jnp.broadcast_to(stat_ref[index : index + 1, :], (expos, LANES))

    matrix = [[None] * NU for _ in range(NU)]
    for index, (u, v) in enumerate(PAIRS):
        plain, once, twice = (value(3 * index + moment) for moment in range(3))
        matrix[u][v] = plain
        matrix[NB + u][v] = once
        matrix[NB + v][u] = once
        matrix[NB + u][NB + v] = twice
    for u in range(2 * NB):
        matrix[2 * NB][u] = value(3 * len(PAIRS) + u)
    pixels = float(rows * tiles * width)
    matrix[2 * NB][2 * NB] = jnp.full((expos, LANES), pixels, jnp.float32)
    trace = matrix[0][0]
    for u in range(1, NU):
        trace = trace + matrix[u][u]
    ridge = RIDGE * (trace / NU)
    for u in range(NU):
        matrix[u][u] = matrix[u][u] + ridge
    right = [stat_ref[count + u * expos : count + (u + 1) * expos, :] for u in range(NU)]
    inverse = [None] * NU
    for j in range(NU):
        inverse[j] = 1.0 / matrix[j][j]
        for i in range(j + 1, NU):
            ratio = matrix[i][j] * inverse[j]
            for m in range(j + 1, i + 1):
                matrix[i][m] = matrix[i][m] - ratio * matrix[m][j]
            right[i] = right[i] - ratio * right[j]
    fitted = [None] * NU
    for j in reversed(range(NU)):
        left = right[j]
        for i in range(j + 1, NU):
            left = left - matrix[i][j] * fitted[i]
        fitted[j] = left * inverse[j]

    spread = lax.broadcasted_iota(jnp.int32, (expos, LANES), 1)
    table = jnp.zeros((expos, LANES), jnp.float32)
    for u in range(NU):
        table = jnp.where(spread == u, fitted[u], table)
    exposure = lax.broadcasted_iota(jnp.int32, (expos, LANES), 0)
    line = jnp.sum(jnp.where(exposure == me, table, 0.0), axis=0, keepdims=True)
    coeffs_ref[0] = line[:, :NU]

    weights = [rbuf[e, tile, :, LANES:] for e in range(expos)]
    stacked = jnp.concatenate(weights, axis=0)
    joint = [jnp.sum(stacked * fitted[u], axis=0, keepdims=True) for u in range(NU)]
    for b, h in chunks:
        result = science_at(0, b, h) * weights[0]
        for e in range(1, expos):
            result = result + science_at(e, b, h) * weights[e]
        result = result - joint[2 * NB]
        for k in range(NB):
            factor = joint[k] + columns[b, h] * joint[NB + k]
            result = result - conv_at(k, b, h) * factor
        start = b * WIDE + h * LANES
        coadd_ref[0, :, start : start + LANES] = result
    for index, e, t in others():
        stat_copy(index, me, tile, e, t).wait_send()


def window(sizes, template, science, plan, orders, coadd_weight, intersection):
    expos, tiles = (sizes["expo"], sizes["tile"])
    rows, width = template.shape[1:]
    cols = width // expos
    fits = (
        science.shape[1] == 1
        and template.shape[0] == 1
        and expos > 1
        and width % expos == 0
        and cols % WIDE == 0
        and rows % 16 == 0
        and 3 * len(PAIRS) + 2 * NB + NU * expos <= LANES
    )
    if not fits:
        return per_device(template, science, plan, orders, coadd_weight, intersection)
    span = cols + 4 * LANES
    dims = (expos, tiles, rows, width, cols)
    dma = pltpu.SemaphoreType.DMA
    anywhere = pl.BlockSpec(memory_space=pl.ANY)
    scalar = pl.BlockSpec(memory_space=pltpu.SMEM)
    vector = pl.BlockSpec(memory_space=pltpu.VMEM)
    return pl.pallas_call(
        functools.partial(fused, dims),
        out_shape=(
            jax.ShapeDtypeStruct((1, rows, cols), jnp.float32),
            jax.ShapeDtypeStruct((1, 1, NU), jnp.float32),
        ),
        in_specs=[anywhere, anywhere, scalar, scalar, scalar, scalar],
        out_specs=(vector, vector),
        scratch_shapes=[
            pltpu.VMEM((expos, 3, rows, span), jnp.bfloat16),
            pltpu.VMEM((expos, rows, cols), jnp.bfloat16),
            pltpu.VMEM((expos, tiles, 1, 2 * LANES), jnp.float32),
            pltpu.VMEM((NB * rows, 3 * rows), jnp.bfloat16),
            pltpu.VMEM((NB, WIDE + 2 * LANES, WIDE), jnp.bfloat16),
            pltpu.VMEM((NB, rows * (cols // WIDE), WIDE), jnp.float32),
            pltpu.VMEM((LANES, LANES), jnp.float32),
            dma((2,)),
            dma((expos,)),
            dma((expos,)),
            dma((expos,)),
            dma((expos,)),
            dma((2, expos)),
            dma((2, expos)),
            dma((expos * tiles,)),
            dma((expos * tiles,)),
        ],
        compiler_params=pltpu.CompilerParams(collective_id=0, has_side_effects=True),
    )(template, science, plan, orders, coadd_weight, intersection)


def solution(mesh):
    return jax.shard_map(
        functools.partial(window, dict(mesh.shape)),
        mesh=mesh,
        in_specs=(
            P(("groups", "expo"), "tile", None),
            P(("groups", "expo"), None, "tile", None),
            P("groups"),
            P(),
            P(("groups", "expo"), None),
            P(("groups", "expo"), None),
        ),
        out_specs=(P("groups", "tile", "expo"), P(("groups", "expo"), None, None)),
        check_vma=False,
    )
```

```python
import functools

import jax
import jax.numpy as jnp
from jax import lax
from jax.experimental import pallas as pl
from jax.experimental.pallas import tpu as pltpu
from jax.sharding import PartitionSpec as P

HALF = 15
NB = 6
NU = 13


SIGMAS = (0.8, 1.4, 2.2, 3.0, 4.0, 5.5)
RIDGE = 0.05


def broadcast(block, axis, holder):
    block = jnp.where(lax.axis_index(axis) == holder, block, jnp.zeros_like(block))
    return lax.psum(block, axis)


def extended(x, sides, width):
    for axis, dim in sides:
        size, length = (lax.axis_size(axis), x.shape[dim])
        up = [(i, (i + 1) % size) for i in range(size - 1)]
        down = [(j, i) for i, j in up]
        last = lax.slice_in_dim(x, length - width, length, axis=dim)
        first = lax.slice_in_dim(x, 0, width, axis=dim)
        before = lax.ppermute(last, axis, up)
        after = lax.ppermute(first, axis, down)
        x = jnp.concatenate([before, x, after], axis=dim)
    return x


def make_filters(orders):
    taps_pos = jnp.arange(2 * HALF + 1).astype(jnp.float32) - HALF
    row_list = []
    col_list = []
    for basis in range(NB):
        sigma = SIGMAS[basis]
        envelope = jnp.exp(-taps_pos * taps_pos / (2.0 * sigma * sigma))

        def power(order):
            return jnp.where(order == 0, 1.0, jnp.where(order == 1, taps_pos, taps_pos * taps_pos))

        row_filter = envelope * power(orders[basis, 0])
        col_filter = envelope * power(orders[basis, 1])
        row_list.append(row_filter / jnp.sqrt(jnp.sum(row_filter * row_filter)))
        col_list.append(col_filter / jnp.sqrt(jnp.sum(col_filter * col_filter)))
    return (jnp.stack(row_list).astype(jnp.bfloat16), jnp.stack(col_list).astype(jnp.bfloat16))


def band_matrix(filters, out_len, in_len):
    offset = jnp.arange(in_len)[None, :] - jnp.arange(out_len)[:, None]
    taps_idx = jnp.arange(2 * HALF + 1)
    picks = (offset[:, :, None] == taps_idx[None, None, :]).astype(jnp.float32)
    band = jnp.einsum("ijt,kt->kij", picks, filters.astype(jnp.float32))
    return band.astype(jnp.bfloat16)


def per_device(template, science, plan, orders, coadd_weight, intersection):
    row_filters, col_filters = make_filters(orders)
    rows = template.shape[1]
    width = template.shape[2]
    blocks_count = width // 128
    steps_count = science.shape[1]
    row_band = band_matrix(row_filters, rows, rows + 2 * HALF)
    col_band = jnp.transpose(band_matrix(col_filters, 128, 128 + 2 * HALF), (0, 2, 1))
    column_pos = 2.0 * (jnp.arange(width).astype(jnp.float32) + 0.5) / width - 1.0
    pieces = []
    fitted = []
    for step in range(steps_count):
        owner_index = plan[step]
        received = broadcast(template[0], "expo", owner_index)
        padded = extended(received, (("tile", 0),), HALF)
        rowconv = jnp.einsum(
            "kij,jw->kiw", row_band, padded, preferred_element_type=jnp.float32
        ).astype(jnp.bfloat16)
        blocks = rowconv.reshape(NB, rows, blocks_count, 128)
        empty_rim = jnp.zeros((NB, rows, 1, HALF), jnp.bfloat16)
        previous = jnp.concatenate([empty_rim, blocks[:, :, :-1, 128 - HALF :]], axis=2)
        following = jnp.concatenate([blocks[:, :, 1:, :HALF], empty_rim], axis=2)
        window = jnp.concatenate([previous, blocks, following], axis=3)
        conv = jnp.einsum("krbj,kjc->krbc", window, col_band, preferred_element_type=jnp.float32)
        conv = conv.reshape(NB, rows, width)
        fields = jnp.concatenate(
            [conv, conv * column_pos, jnp.ones((1, rows, width), jnp.float32)], axis=0
        )
        fields = fields.reshape(NU, rows * width)
        exposure_image = science[0, step].astype(jnp.float32).reshape(rows * width)
        normal_local = jnp.dot(fields, fields.T, precision=lax.Precision.HIGHEST)
        project_local = jnp.dot(fields, exposure_image, precision=lax.Precision.HIGHEST)
        normal_matrix, projections = lax.psum((normal_local, project_local), "tile")
        normal_matrix = normal_matrix + RIDGE * (jnp.trace(normal_matrix) / NU) * jnp.eye(
            NU, dtype=jnp.float32
        )
        factor = jnp.linalg.cholesky(normal_matrix)
        coeffs = jax.scipy.linalg.cho_solve((factor, True), projections)
        model = jnp.dot(coeffs, fields, precision=lax.Precision.HIGHEST)
        difference = exposure_image - model
        weight_now = coadd_weight[0, step] * intersection[0, step].astype(jnp.float32)
        pieces.append((weight_now * difference).reshape(rows, width))
        fitted.append(coeffs)
    weighted = jnp.stack(pieces)
    received_parts = lax.all_to_all(weighted[None], "expo", split_axis=3, concat_axis=0, tiled=True)
    coadd = jnp.sum(received_parts, axis=0)
    return (coadd, jnp.stack(fitted)[None])


LANES = 128
VMEM_BYTES = 67043328
WIDE = 256
PAIRS = [(u, v) for u in range(NB) for v in range(u + 1)]
MESH = pl.DeviceIdType.MESH


def taps(position, sigma, order):
    power = jnp.where(order == 0, 1.0, jnp.where(order == 1, position, position * position))
    value = jnp.exp(-position * position / (2.0 * sigma * sigma)) * power
    return jnp.where(jnp.abs(position) <= HALF, value, 0.0)


def fused(
    dims,
    template_ref,
    science_ref,
    plan_ref,
    orders_ref,
    weight_ref,
    inter_ref,
    coadd_ref,
    coeffs_ref,
    tbuf,
    sbuf,
    rbuf,
    row_band,
    col_band,
    conv_ref,
    stat_ref,
    local_sem,
    tsend,
    trecv,
    ssend,
    srecv,
    fsend,
    frecv,
    rsend,
    rrecv,
):
    expos, tiles, rows, width, cols = dims
    per = cols // LANES
    span = cols + 2 * LANES
    blocks = cols // WIDE
    chunks = [(b, h) for b in range(blocks) for h in range(WIDE // LANES)]
    me = lax.axis_index("expo")
    tile = lax.axis_index("tile")

    def others():
        for de in range(expos):
            for dt in range(tiles):
                if de or dt:
                    yield de * tiles + dt, (me + de) % expos, (tile + dt) % tiles

    barrier = pltpu.get_barrier_semaphore()
    for d in range(1, expos):
        peer = (me + d) % expos
        pl.semaphore_signal(barrier, inc=1, device_id={"expo": peer}, device_id_type=MESH)
    for d in (1, tiles - 1):
        peer = (tile + d) % tiles
        pl.semaphore_signal(barrier, inc=1, device_id={"tile": peer}, device_id_type=MESH)

    def source_start(e):
        return e * per - 1 + (expos - 1 - e) // (expos - 1) - e // (expos - 1)

    def source_columns(e):
        return pl.ds(pl.multiple_of(source_start(e) * LANES, LANES), span)

    def window_columns(e):
        return pl.ds(pl.multiple_of((source_start(e) - e * per + 2) * LANES, LANES), span)

    def own_columns(e):
        return pl.ds(pl.multiple_of(e * cols, LANES), cols)

    mine = pltpu.make_async_copy(
        template_ref.at[0, :, source_columns(me)],
        tbuf.at[me, 1, :, window_columns(me)],
        local_sem.at[0],
    )
    mine.start()
    mine_science = pltpu.make_async_copy(
        science_ref.at[0, 0, :, own_columns(me)], sbuf.at[me], local_sem.at[1]
    )
    mine_science.start()

    def template_copy(d, target, holder):
        return pltpu.make_async_remote_copy(
            src_ref=template_ref.at[0, :, source_columns(target)],
            dst_ref=tbuf.at[holder, 1, :, window_columns(target)],
            send_sem=tsend.at[d],
            recv_sem=trecv.at[d],
            device_id={"expo": target},
            device_id_type=MESH,
        )

    def science_copy(d, target, holder):
        return pltpu.make_async_remote_copy(
            src_ref=science_ref.at[0, 0, :, own_columns(target)],
            dst_ref=sbuf.at[holder],
            send_sem=ssend.at[d],
            recv_sem=srecv.at[d],
            device_id={"expo": target},
            device_id_type=MESH,
        )

    def forward_copy(d, holder, side):
        target = tile + 1 if side == 0 else tile - 1
        return pltpu.make_async_remote_copy(
            src_ref=tbuf.at[holder, 1, :, window_columns(me)],
            dst_ref=tbuf.at[holder, 2 * side, :, window_columns(me)],
            send_sem=fsend.at[side, d],
            recv_sem=frecv.at[side, d],
            device_id={"tile": target},
            device_id_type=MESH,
        )

    def forward(d, holder):
        @pl.when(tile < tiles - 1)
        def _():
            forward_copy(d, holder, 0).start()

        @pl.when(tile > 0)
        def _():
            forward_copy(d, holder, 1).start()

    position = lax.broadcasted_iota(jnp.int32, (1, LANES), 1).astype(jnp.float32) - HALF
    for k in range(NB):
        sigma = SIGMAS[k]
        for side, length in ((0, rows), (1, LANES)):
            order = jnp.full((1, LANES), orders_ref[side, k], jnp.int32)
            line = taps(position, sigma, order)
            root = jnp.sqrt(jnp.sum(line * line, axis=1, keepdims=True))
            scale = 1.0 / root
            if side == 0:
                shape = (rows, 3 * rows)
                offset = (
                    lax.broadcasted_iota(jnp.int32, shape, 1)
                    - lax.broadcasted_iota(jnp.int32, shape, 0)
                    - rows
                ).astype(jnp.float32)
                band = taps(offset, sigma, jnp.full(shape, orders_ref[side, k], jnp.int32))
                row_band[k * rows : (k + 1) * rows, :] = (band * scale).astype(jnp.bfloat16)
            else:
                shape = (LANES, LANES)
                delta = lax.broadcasted_iota(jnp.int32, shape, 0) - lax.broadcasted_iota(
                    jnp.int32, shape, 1
                )
                column_order = jnp.full(shape, orders_ref[side, k], jnp.int32)
                zero = jnp.zeros(shape, jnp.bfloat16)
                parts = {}
                for kind in range(3):
                    offset = (delta + (kind - 1) * LANES).astype(jnp.float32)
                    band = taps(offset, sigma, column_order)
                    parts[kind] = (band * scale).astype(jnp.bfloat16)
                for jb in range(WIDE // LANES + 2):
                    for cb in range(WIDE // LANES):
                        col_band[
                            k,
                            jb * LANES : (jb + 1) * LANES,
                            cb * LANES : (cb + 1) * LANES,
                        ] = parts.get(jb - cb, zero)

    pl.semaphore_wait(barrier, expos + 1)
    for d in range(1, expos):
        template_copy(d, (me + d) % expos, me).start()
    mine.wait()
    forward(0, me)
    for d in range(1, expos):
        science_copy(d, (me + d) % expos, me).start()

    for d in range(1, expos):
        holder = (me + expos - d) % expos
        template_copy(d, me, holder).wait_recv()
        forward(d, holder)

    @pl.when(tile > 0)
    def _():
        for d in range(expos):
            forward_copy(d, (me + expos - d) % expos, 0).wait_recv()

    @pl.when(tile < tiles - 1)
    def _():
        for d in range(expos):
            forward_copy(d, (me + expos - d) % expos, 1).wait_recv()

    @pl.when(tile < tiles - 1)
    def _():
        for d in range(expos):
            forward_copy(d, (me + expos - d) % expos, 0).wait_send()

    @pl.when(tile > 0)
    def _():
        for d in range(expos):
            forward_copy(d, (me + expos - d) % expos, 1).wait_send()

    owner = plan_ref[0]
    shape = (rows, span)
    column = lax.broadcasted_iota(jnp.int32, shape, 1) + (me * cols - LANES)
    inside = (column >= 0) & (column < width)
    pieces = []
    for part in range(3):
        block = tbuf[owner, part, :, LANES : LANES + span].astype(jnp.float32)
        keep = inside
        if part == 0:
            keep = keep & (jnp.full(shape, tile, jnp.int32) > 0)
        if part == 2:
            keep = keep & (jnp.full(shape, tile, jnp.int32) < tiles - 1)
        pieces.append(jnp.where(keep, block, 0.0).astype(jnp.bfloat16))
    rows_window = jnp.concatenate(pieces, axis=0)
    rowconv = jnp.dot(
        row_band[...], rows_window, preferred_element_type=jnp.float32
    ).astype(jnp.bfloat16)
    for k in range(NB):
        mine_rows = rowconv[k * rows : (k + 1) * rows]
        windows = jnp.concatenate(
            [mine_rows[:, b * WIDE : (b + 1) * WIDE + 2 * LANES] for b in range(blocks)], axis=0
        )
        conv_ref[k] = jnp.dot(windows, col_band[k], preferred_element_type=jnp.float32)

    def conv_at(k, b, h):
        return conv_ref[k, b * rows : (b + 1) * rows, h * LANES : (h + 1) * LANES]

    def science_at(e, b, h):
        start = b * WIDE + h * LANES
        return sbuf[e, :, start : start + LANES].astype(jnp.float32)

    def fold(x):
        return x.reshape(rows // 8, 8, LANES).sum(axis=0)

    lane = lax.broadcasted_iota(jnp.int32, (1, LANES), 1)
    columns = {}
    for b, h in chunks:
        place = (me * cols + b * WIDE + h * LANES + lane).astype(jnp.float32)
        columns[b, h] = 2.0 * (place + 0.5) / width - 1.0

    def put(index, value):
        stat_ref[index : index + 1, :] = jnp.sum(value, axis=0, keepdims=True)

    count = 3 * len(PAIRS) + 2 * NB
    for index, (u, v) in enumerate(PAIRS):
        sums = [0.0, 0.0, 0.0]
        for b, h in chunks:
            product = fold(conv_at(u, b, h) * conv_at(v, b, h))
            once = product * columns[b, h]
            sums = [sums[0] + product, sums[1] + once, sums[2] + once * columns[b, h]]
        for moment in range(3):
            put(3 * index + moment, sums[moment])
    for u in range(NB):
        sums = [0.0, 0.0]
        for b, h in chunks:
            product = fold(conv_at(u, b, h))
            sums = [sums[0] + product, sums[1] + product * columns[b, h]]
        for moment in range(2):
            put(3 * len(PAIRS) + NB * moment + u, sums[moment])

    mine_science.wait()
    for d in range(1, expos):
        science_copy(d, me, (me + expos - d) % expos).wait_recv()
    for e in range(expos):
        for u in range(NB):
            sums = [0.0, 0.0]
            for b, h in chunks:
                product = fold(conv_at(u, b, h) * science_at(e, b, h))
                sums = [sums[0] + product, sums[1] + product * columns[b, h]]
            for moment in range(2):
                put(count + (NB * moment + u) * expos + e, sums[moment])
        total = 0.0
        for b, h in chunks:
            total = total + fold(science_at(e, b, h))
        put(count + 2 * NB * expos + e, total)
    used = count + NU * expos
    if used < LANES:
        stat_ref[used:LANES, :] = jnp.zeros((LANES - used, LANES), jnp.float32)

    reduced = jnp.sum(jnp.transpose(stat_ref[...]), axis=0, keepdims=True)
    weight = weight_ref[0] * inter_ref[0].astype(jnp.float32)
    rbuf[me, tile, :, :LANES] = reduced
    rbuf[me, tile, :, LANES:] = jnp.full((1, LANES), weight, jnp.float32)

    def stat_copy(index, e, t, to_e, to_t):
        return pltpu.make_async_remote_copy(
            src_ref=rbuf.at[e, t],
            dst_ref=rbuf.at[e, t],
            send_sem=rsend.at[index],
            recv_sem=rrecv.at[index],
            device_id={"expo": to_e, "tile": to_t},
            device_id_type=MESH,
        )

    for index, e, t in others():
        stat_copy(index, me, tile, e, t).start()
    for d in range(1, expos):
        template_copy(d, (me + d) % expos, me).wait_send()
        science_copy(d, (me + d) % expos, me).wait_send()
    for de in range(expos):
        for dt in range(tiles):
            if de or dt:
                e = (me + expos - de) % expos
                t = (tile + tiles - dt) % tiles
                stat_copy(de * tiles + dt, e, t, e, t).wait_recv()

    total = rbuf[0, 0, :, :LANES]
    for e in range(expos):
        for t in range(tiles):
            if e or t:
                total = total + rbuf[e, t, :, :LANES]
    stat_ref[...] = jnp.transpose(jnp.broadcast_to(total, (LANES, LANES)))

    def value(index):
        return jnp.broadcast_to(stat_ref[index : index + 1, :], (expos, LANES))

    matrix = [[None] * NU for _ in range(NU)]
    for index, (u, v) in enumerate(PAIRS):
        plain, once, twice = (value(3 * index + moment) for moment in range(3))
        matrix[u][v] = plain
        matrix[NB + u][v] = once
        matrix[NB + v][u] = once
        matrix[NB + u][NB + v] = twice
    for u in range(2 * NB):
        matrix[2 * NB][u] = value(3 * len(PAIRS) + u)
    pixels = float(rows * tiles * width)
    matrix[2 * NB][2 * NB] = jnp.full((expos, LANES), pixels, jnp.float32)
    trace = matrix[0][0]
    for u in range(1, NU):
        trace = trace + matrix[u][u]
    ridge = RIDGE * (trace / NU)
    for u in range(NU):
        matrix[u][u] = matrix[u][u] + ridge
    right = [stat_ref[count + u * expos : count + (u + 1) * expos, :] for u in range(NU)]
    inverse = [None] * NU
    for j in range(NU):
        inverse[j] = 1.0 / matrix[j][j]
        for i in range(j + 1, NU):
            ratio = matrix[i][j] * inverse[j]
            for m in range(j + 1, i + 1):
                matrix[i][m] = matrix[i][m] - ratio * matrix[m][j]
            right[i] = right[i] - ratio * right[j]
    fitted = [None] * NU
    for j in reversed(range(NU)):
        left = right[j]
        for i in range(j + 1, NU):
            left = left - matrix[i][j] * fitted[i]
        fitted[j] = left * inverse[j]

    spread = lax.broadcasted_iota(jnp.int32, (expos, LANES), 1)
    table = jnp.zeros((expos, LANES), jnp.float32)
    for u in range(NU):
        table = jnp.where(spread == u, fitted[u], table)
    exposure = lax.broadcasted_iota(jnp.int32, (expos, LANES), 0)
    line = jnp.sum(jnp.where(exposure == me, table, 0.0), axis=0, keepdims=True)
    coeffs_ref[0] = line[:, :NU]

    weights = [rbuf[e, tile, :, LANES:] for e in range(expos)]
    stacked = jnp.concatenate(weights, axis=0)
    joint = [jnp.sum(stacked * fitted[u], axis=0, keepdims=True) for u in range(NU)]
    for b, h in chunks:
        result = science_at(0, b, h) * weights[0]
        for e in range(1, expos):
            result = result + science_at(e, b, h) * weights[e]
        result = result - joint[2 * NB]
        for k in range(NB):
            factor = joint[k] + columns[b, h] * joint[NB + k]
            result = result - conv_at(k, b, h) * factor
        start = b * WIDE + h * LANES
        coadd_ref[0, :, start : start + LANES] = result
    for index, e, t in others():
        stat_copy(index, me, tile, e, t).wait_send()


def window(sizes, template, science, plan, orders, coadd_weight, intersection):
    expos, tiles = (sizes["expo"], sizes["tile"])
    rows, width = template.shape[1:]
    cols = width // expos
    fits = (
        science.shape[1] == 1
        and template.shape[0] == 1
        and expos > 1
        and tiles > 1
        and width % expos == 0
        and cols % WIDE == 0
        and rows % 16 == 0
        and 3 * len(PAIRS) + 2 * NB + NU * expos <= LANES
    )
    if not fits:
        return per_device(template, science, plan, orders, coadd_weight, intersection)
    span = cols + 4 * LANES
    spare = 4 * rows * cols + (1 << 14)
    dims = (expos, tiles, rows, width, cols)
    dma = pltpu.SemaphoreType.DMA
    scalar = pl.BlockSpec(memory_space=pltpu.SMEM)
    far = pl.BlockSpec(memory_space=pltpu.HBM)
    vector = pl.BlockSpec(memory_space=pltpu.VMEM)
    return pl.pallas_call(
        functools.partial(fused, dims),
        out_shape=(
            jax.ShapeDtypeStruct((1, rows, cols), jnp.float32),
            jax.ShapeDtypeStruct((1, 1, NU), jnp.float32),
        ),
        in_specs=[far, far, scalar, scalar, scalar, scalar],
        out_specs=(vector, vector),
        scratch_shapes=[
            pltpu.VMEM((expos, 3, rows, span), jnp.bfloat16),
            pltpu.VMEM((expos, rows, cols), jnp.bfloat16),
            pltpu.VMEM((expos, tiles, 1, 2 * LANES), jnp.float32),
            pltpu.VMEM((NB * rows, 3 * rows), jnp.bfloat16),
            pltpu.VMEM((NB, WIDE + 2 * LANES, WIDE), jnp.bfloat16),
            pltpu.VMEM((NB, rows * (cols // WIDE), WIDE), jnp.float32),
            pltpu.VMEM((LANES, LANES), jnp.float32),
            dma((2,)),
            dma((expos,)),
            dma((expos,)),
            dma((expos,)),
            dma((expos,)),
            dma((2, expos)),
            dma((2, expos)),
            dma((expos * tiles,)),
            dma((expos * tiles,)),
        ],
        compiler_params=pltpu.CompilerParams(collective_id=0, has_side_effects=True, vmem_limit_bytes=VMEM_BYTES - spare),
    )(template, science, plan, orders.T, coadd_weight[0], intersection[0])


def solution(mesh):
    return jax.shard_map(
        functools.partial(window, dict(mesh.shape)),
        mesh=mesh,
        in_specs=(
            P(("groups", "expo"), "tile", None),
            P(("groups", "expo"), None, "tile", None),
            P("groups"),
            P(),
            P(("groups", "expo"), None),
            P(("groups", "expo"), None),
        ),
        out_specs=(P("groups", "tile", "expo"), P(("groups", "expo"), None, None)),
        check_vma=False,
    )
```

```python
import functools

import jax
import jax.numpy as jnp
from jax import lax
from jax.experimental import pallas as pl
from jax.experimental.pallas import tpu as pltpu
from jax.sharding import PartitionSpec as P

HALF = 15
NB = 6
NU = 13


SIGMAS = (0.8, 1.4, 2.2, 3.0, 4.0, 5.5)
RIDGE = 0.05


def broadcast(block, axis, holder):
    block = jnp.where(lax.axis_index(axis) == holder, block, jnp.zeros_like(block))
    return lax.psum(block, axis)


def extended(x, sides, width):
    for axis, dim in sides:
        size, length = (lax.axis_size(axis), x.shape[dim])
        up = [(i, (i + 1) % size) for i in range(size - 1)]
        down = [(j, i) for i, j in up]
        last = lax.slice_in_dim(x, length - width, length, axis=dim)
        first = lax.slice_in_dim(x, 0, width, axis=dim)
        before = lax.ppermute(last, axis, up)
        after = lax.ppermute(first, axis, down)
        x = jnp.concatenate([before, x, after], axis=dim)
    return x


def make_filters(orders):
    taps_pos = jnp.arange(2 * HALF + 1).astype(jnp.float32) - HALF
    row_list = []
    col_list = []
    for basis in range(NB):
        sigma = SIGMAS[basis]
        envelope = jnp.exp(-taps_pos * taps_pos / (2.0 * sigma * sigma))

        def power(order):
            return jnp.where(order == 0, 1.0, jnp.where(order == 1, taps_pos, taps_pos * taps_pos))

        row_filter = envelope * power(orders[basis, 0])
        col_filter = envelope * power(orders[basis, 1])
        row_list.append(row_filter / jnp.sqrt(jnp.sum(row_filter * row_filter)))
        col_list.append(col_filter / jnp.sqrt(jnp.sum(col_filter * col_filter)))
    return (jnp.stack(row_list).astype(jnp.bfloat16), jnp.stack(col_list).astype(jnp.bfloat16))


def band_matrix(filters, out_len, in_len):
    offset = jnp.arange(in_len)[None, :] - jnp.arange(out_len)[:, None]
    taps_idx = jnp.arange(2 * HALF + 1)
    picks = (offset[:, :, None] == taps_idx[None, None, :]).astype(jnp.float32)
    band = jnp.einsum("ijt,kt->kij", picks, filters.astype(jnp.float32))
    return band.astype(jnp.bfloat16)


def per_device(template, science, plan, orders, coadd_weight, intersection):
    row_filters, col_filters = make_filters(orders)
    rows = template.shape[1]
    width = template.shape[2]
    blocks_count = width // 128
    steps_count = science.shape[1]
    row_band = band_matrix(row_filters, rows, rows + 2 * HALF)
    col_band = jnp.transpose(band_matrix(col_filters, 128, 128 + 2 * HALF), (0, 2, 1))
    column_pos = 2.0 * (jnp.arange(width).astype(jnp.float32) + 0.5) / width - 1.0
    pieces = []
    fitted = []
    for step in range(steps_count):
        owner_index = plan[step]
        received = broadcast(template[0], "expo", owner_index)
        padded = extended(received, (("tile", 0),), HALF)
        rowconv = jnp.einsum(
            "kij,jw->kiw", row_band, padded, preferred_element_type=jnp.float32
        ).astype(jnp.bfloat16)
        blocks = rowconv.reshape(NB, rows, blocks_count, 128)
        empty_rim = jnp.zeros((NB, rows, 1, HALF), jnp.bfloat16)
        previous = jnp.concatenate([empty_rim, blocks[:, :, :-1, 128 - HALF :]], axis=2)
        following = jnp.concatenate([blocks[:, :, 1:, :HALF], empty_rim], axis=2)
        window = jnp.concatenate([previous, blocks, following], axis=3)
        conv = jnp.einsum("krbj,kjc->krbc", window, col_band, preferred_element_type=jnp.float32)
        conv = conv.reshape(NB, rows, width)
        fields = jnp.concatenate(
            [conv, conv * column_pos, jnp.ones((1, rows, width), jnp.float32)], axis=0
        )
        fields = fields.reshape(NU, rows * width)
        exposure_image = science[0, step].astype(jnp.float32).reshape(rows * width)
        normal_local = jnp.dot(fields, fields.T, precision=lax.Precision.HIGHEST)
        project_local = jnp.dot(fields, exposure_image, precision=lax.Precision.HIGHEST)
        normal_matrix, projections = lax.psum((normal_local, project_local), "tile")
        normal_matrix = normal_matrix + RIDGE * (jnp.trace(normal_matrix) / NU) * jnp.eye(
            NU, dtype=jnp.float32
        )
        factor = jnp.linalg.cholesky(normal_matrix)
        coeffs = jax.scipy.linalg.cho_solve((factor, True), projections)
        model = jnp.dot(coeffs, fields, precision=lax.Precision.HIGHEST)
        difference = exposure_image - model
        weight_now = coadd_weight[0, step] * intersection[0, step].astype(jnp.float32)
        pieces.append((weight_now * difference).reshape(rows, width))
        fitted.append(coeffs)
    weighted = jnp.stack(pieces)
    received_parts = lax.all_to_all(weighted[None], "expo", split_axis=3, concat_axis=0, tiled=True)
    coadd = jnp.sum(received_parts, axis=0)
    return (coadd, jnp.stack(fitted)[None])


LANES = 128
VMEM_BYTES = 67043328
WIDE = 256
PAIRS = [(u, v) for u in range(NB) for v in range(u + 1)]
MESH = pl.DeviceIdType.MESH


def taps(position, sigma, order):
    power = jnp.where(order == 0, 1.0, jnp.where(order == 1, position, position * position))
    value = jnp.exp(-position * position / (2.0 * sigma * sigma)) * power
    return jnp.where(jnp.abs(position) <= HALF, value, 0.0)


def fused(
    dims,
    template_ref,
    science_ref,
    plan_ref,
    orders_ref,
    weight_ref,
    inter_ref,
    coadd_ref,
    coeffs_ref,
    tbuf,
    sbuf,
    rbuf,
    row_band,
    col_band,
    conv_ref,
    stat_ref,
    local_sem,
    tsend,
    trecv,
    ssend,
    srecv,
    fsend,
    frecv,
    rsend,
    rrecv,
):
    expos, tiles, rows, width, cols = dims
    per = cols // LANES
    span = cols + 2 * LANES
    blocks = cols // WIDE
    chunks = [(b, h) for b in range(blocks) for h in range(WIDE // LANES)]
    me = lax.axis_index("expo")
    tile = lax.axis_index("tile")

    def others():
        for de in range(expos):
            for dt in range(tiles):
                if de or dt:
                    yield de * tiles + dt, (me + de) % expos, (tile + dt) % tiles

    barrier = pltpu.get_barrier_semaphore()
    for d in range(1, expos):
        peer = (me + d) % expos
        pl.semaphore_signal(barrier, inc=1, device_id={"expo": peer}, device_id_type=MESH)
    for d in (1, tiles - 1):
        peer = (tile + d) % tiles
        pl.semaphore_signal(barrier, inc=1, device_id={"tile": peer}, device_id_type=MESH)

    def source_start(e):
        return e * per - 1 + (expos - 1 - e) // (expos - 1) - e // (expos - 1)

    def source_columns(e):
        return pl.ds(pl.multiple_of(source_start(e) * LANES, LANES), span)

    def window_columns(e):
        return pl.ds(pl.multiple_of((source_start(e) - e * per + 2) * LANES, LANES), span)

    def own_columns(e):
        return pl.ds(pl.multiple_of(e * cols, LANES), cols)

    mine = pltpu.make_async_copy(
        template_ref.at[0, :, source_columns(me)],
        tbuf.at[me, 1, :, window_columns(me)],
        local_sem.at[0],
    )
    mine.start()
    mine_science = pltpu.make_async_copy(
        science_ref.at[0, 0, :, own_columns(me)], sbuf.at[me], local_sem.at[1]
    )
    mine_science.start()

    def template_copy(d, target, holder):
        return pltpu.make_async_remote_copy(
            src_ref=template_ref.at[0, :, source_columns(target)],
            dst_ref=tbuf.at[holder, 1, :, window_columns(target)],
            send_sem=tsend.at[d],
            recv_sem=trecv.at[d],
            device_id={"expo": target},
            device_id_type=MESH,
        )

    def science_copy(d, target, holder):
        return pltpu.make_async_remote_copy(
            src_ref=science_ref.at[0, 0, :, own_columns(target)],
            dst_ref=sbuf.at[holder],
            send_sem=ssend.at[d],
            recv_sem=srecv.at[d],
            device_id={"expo": target},
            device_id_type=MESH,
        )

    def forward_copy(d, holder, side):
        target = tile + 1 if side == 0 else tile - 1
        return pltpu.make_async_remote_copy(
            src_ref=tbuf.at[holder, 1, :, window_columns(me)],
            dst_ref=tbuf.at[holder, 2 * side, :, window_columns(me)],
            send_sem=fsend.at[side, d],
            recv_sem=frecv.at[side, d],
            device_id={"tile": target},
            device_id_type=MESH,
        )

    def forward(d, holder):
        @pl.when(tile < tiles - 1)
        def _():
            forward_copy(d, holder, 0).start()

        @pl.when(tile > 0)
        def _():
            forward_copy(d, holder, 1).start()

    position = lax.broadcasted_iota(jnp.int32, (1, LANES), 1).astype(jnp.float32) - HALF
    for k in range(NB):
        sigma = SIGMAS[k]
        for side, length in ((0, rows), (1, LANES)):
            order = jnp.full((1, LANES), orders_ref[side, k], jnp.int32)
            line = taps(position, sigma, order)
            root = jnp.sqrt(jnp.sum(line * line, axis=1, keepdims=True))
            scale = 1.0 / root
            if side == 0:
                shape = (rows, 3 * rows)
                offset = (
                    lax.broadcasted_iota(jnp.int32, shape, 1)
                    - lax.broadcasted_iota(jnp.int32, shape, 0)
                    - rows
                ).astype(jnp.float32)
                band = taps(offset, sigma, jnp.full(shape, orders_ref[side, k], jnp.int32))
                row_band[k * rows : (k + 1) * rows, :] = (band * scale).astype(jnp.bfloat16)
            else:
                shape = (LANES, LANES)
                delta = lax.broadcasted_iota(jnp.int32, shape, 0) - lax.broadcasted_iota(
                    jnp.int32, shape, 1
                )
                column_order = jnp.full(shape, orders_ref[side, k], jnp.int32)
                zero = jnp.zeros(shape, jnp.bfloat16)
                parts = {}
                for kind in range(3):
                    offset = (delta + (kind - 1) * LANES).astype(jnp.float32)
                    band = taps(offset, sigma, column_order)
                    parts[kind] = (band * scale).astype(jnp.bfloat16)
                for jb in range(WIDE // LANES + 2):
                    for cb in range(WIDE // LANES):
                        col_band[
                            k,
                            jb * LANES : (jb + 1) * LANES,
                            cb * LANES : (cb + 1) * LANES,
                        ] = parts.get(jb - cb, zero)

    pl.semaphore_wait(barrier, expos + 1)
    for d in range(1, expos):
        template_copy(d, (me + d) % expos, me).start()
    mine.wait()
    forward(0, me)
    for d in range(1, expos):
        science_copy(d, (me + d) % expos, me).start()

    for d in range(1, expos):
        holder = (me + expos - d) % expos
        template_copy(d, me, holder).wait_recv()
        forward(d, holder)

    @pl.when(tile > 0)
    def _():
        for d in range(expos):
            forward_copy(d, (me + expos - d) % expos, 0).wait_recv()

    @pl.when(tile < tiles - 1)
    def _():
        for d in range(expos):
            forward_copy(d, (me + expos - d) % expos, 1).wait_recv()

    @pl.when(tile < tiles - 1)
    def _():
        for d in range(expos):
            forward_copy(d, (me + expos - d) % expos, 0).wait_send()

    @pl.when(tile > 0)
    def _():
        for d in range(expos):
            forward_copy(d, (me + expos - d) % expos, 1).wait_send()

    owner = plan_ref[0]
    shape = (rows, span)
    column = lax.broadcasted_iota(jnp.int32, shape, 1) + (me * cols - LANES)
    inside = (column >= 0) & (column < width)
    pieces = []
    for part in range(3):
        block = tbuf[owner, part, :, LANES : LANES + span].astype(jnp.float32)
        keep = inside
        if part == 0:
            keep = keep & (jnp.full(shape, tile, jnp.int32) > 0)
        if part == 2:
            keep = keep & (jnp.full(shape, tile, jnp.int32) < tiles - 1)
        pieces.append(jnp.where(keep, block, 0.0).astype(jnp.bfloat16))
    rows_window = jnp.concatenate(pieces, axis=0)
    rowconv = jnp.dot(
        row_band[...], rows_window, preferred_element_type=jnp.float32
    ).astype(jnp.bfloat16)
    for k in range(NB):
        mine_rows = rowconv[k * rows : (k + 1) * rows]
        windows = jnp.concatenate(
            [mine_rows[:, b * WIDE : (b + 1) * WIDE + 2 * LANES] for b in range(blocks)], axis=0
        )
        conv_ref[k] = jnp.dot(windows, col_band[k], preferred_element_type=jnp.float32)

    def conv_at(k, b, h):
        return conv_ref[k, b * rows : (b + 1) * rows, h * LANES : (h + 1) * LANES]

    def science_at(e, b, h):
        start = b * WIDE + h * LANES
        return sbuf[e, :, start : start + LANES].astype(jnp.float32)

    def fold(x):
        return x.reshape(rows // 8, 8, LANES).sum(axis=0)

    lane = lax.broadcasted_iota(jnp.int32, (1, LANES), 1)
    columns = {}
    for b, h in chunks:
        place = (me * cols + b * WIDE + h * LANES + lane).astype(jnp.float32)
        columns[b, h] = 2.0 * (place + 0.5) / width - 1.0

    def put(index, value):
        stat_ref[index : index + 1, :] = jnp.sum(value, axis=0, keepdims=True)

    count = 3 * len(PAIRS) + 2 * NB
    for index, (u, v) in enumerate(PAIRS):
        sums = [0.0, 0.0, 0.0]
        for b, h in chunks:
            product = fold(conv_at(u, b, h) * conv_at(v, b, h))
            once = product * columns[b, h]
            sums = [sums[0] + product, sums[1] + once, sums[2] + once * columns[b, h]]
        for moment in range(3):
            put(3 * index + moment, sums[moment])
    for u in range(NB):
        sums = [0.0, 0.0]
        for b, h in chunks:
            product = fold(conv_at(u, b, h))
            sums = [sums[0] + product, sums[1] + product * columns[b, h]]
        for moment in range(2):
            put(3 * len(PAIRS) + NB * moment + u, sums[moment])

    mine_science.wait()
    for d in range(1, expos):
        science_copy(d, me, (me + expos - d) % expos).wait_recv()
    for e in range(expos):
        for u in range(NB):
            sums = [0.0, 0.0]
            for b, h in chunks:
                product = fold(conv_at(u, b, h) * science_at(e, b, h))
                sums = [sums[0] + product, sums[1] + product * columns[b, h]]
            for moment in range(2):
                put(count + (NB * moment + u) * expos + e, sums[moment])
        total = 0.0
        for b, h in chunks:
            total = total + fold(science_at(e, b, h))
        put(count + 2 * NB * expos + e, total)
    used = count + NU * expos
    if used < LANES:
        stat_ref[used:LANES, :] = jnp.zeros((LANES - used, LANES), jnp.float32)

    reduced = jnp.sum(jnp.transpose(stat_ref[...]), axis=0, keepdims=True)
    weight = weight_ref[...] * inter_ref[...].astype(jnp.float32)
    rbuf[me, tile, :, :LANES] = reduced
    rbuf[me, tile, :, LANES:] = jnp.broadcast_to(weight, (1, LANES))

    def stat_copy(index, e, t, to_e, to_t):
        return pltpu.make_async_remote_copy(
            src_ref=rbuf.at[e, t],
            dst_ref=rbuf.at[e, t],
            send_sem=rsend.at[index],
            recv_sem=rrecv.at[index],
            device_id={"expo": to_e, "tile": to_t},
            device_id_type=MESH,
        )

    for index, e, t in others():
        stat_copy(index, me, tile, e, t).start()
    for d in range(1, expos):
        template_copy(d, (me + d) % expos, me).wait_send()
        science_copy(d, (me + d) % expos, me).wait_send()
    for de in range(expos):
        for dt in range(tiles):
            if de or dt:
                e = (me + expos - de) % expos
                t = (tile + tiles - dt) % tiles
                stat_copy(de * tiles + dt, e, t, e, t).wait_recv()

    total = rbuf[0, 0, :, :LANES]
    for e in range(expos):
        for t in range(tiles):
            if e or t:
                total = total + rbuf[e, t, :, :LANES]
    stat_ref[...] = jnp.transpose(jnp.broadcast_to(total, (LANES, LANES)))

    def value(index):
        return jnp.broadcast_to(stat_ref[index : index + 1, :], (expos, LANES))

    matrix = [[None] * NU for _ in range(NU)]
    for index, (u, v) in enumerate(PAIRS):
        plain, once, twice = (value(3 * index + moment) for moment in range(3))
        matrix[u][v] = plain
        matrix[NB + u][v] = once
        matrix[NB + v][u] = once
        matrix[NB + u][NB + v] = twice
    for u in range(2 * NB):
        matrix[2 * NB][u] = value(3 * len(PAIRS) + u)
    pixels = float(rows * tiles * width)
    matrix[2 * NB][2 * NB] = jnp.full((expos, LANES), pixels, jnp.float32)
    trace = matrix[0][0]
    for u in range(1, NU):
        trace = trace + matrix[u][u]
    ridge = RIDGE * (trace / NU)
    for u in range(NU):
        matrix[u][u] = matrix[u][u] + ridge
    right = [stat_ref[count + u * expos : count + (u + 1) * expos, :] for u in range(NU)]
    inverse = [None] * NU
    for j in range(NU):
        inverse[j] = 1.0 / matrix[j][j]
        for i in range(j + 1, NU):
            ratio = matrix[i][j] * inverse[j]
            for m in range(j + 1, i + 1):
                matrix[i][m] = matrix[i][m] - ratio * matrix[m][j]
            right[i] = right[i] - ratio * right[j]
    fitted = [None] * NU
    for j in reversed(range(NU)):
        left = right[j]
        for i in range(j + 1, NU):
            left = left - matrix[i][j] * fitted[i]
        fitted[j] = left * inverse[j]

    spread = lax.broadcasted_iota(jnp.int32, (expos, LANES), 1)
    table = jnp.zeros((expos, LANES), jnp.float32)
    for u in range(NU):
        table = jnp.where(spread == u, fitted[u], table)
    exposure = lax.broadcasted_iota(jnp.int32, (expos, LANES), 0)
    line = jnp.sum(jnp.where(exposure == me, table, 0.0), axis=0, keepdims=True)
    coeffs_ref[0] = line[:, :NU]

    weights = [rbuf[e, tile, :, LANES:] for e in range(expos)]
    stacked = jnp.concatenate(weights, axis=0)
    joint = [jnp.sum(stacked * fitted[u], axis=0, keepdims=True) for u in range(NU)]
    for b, h in chunks:
        result = science_at(0, b, h) * weights[0]
        for e in range(1, expos):
            result = result + science_at(e, b, h) * weights[e]
        result = result - joint[2 * NB]
        for k in range(NB):
            factor = joint[k] + columns[b, h] * joint[NB + k]
            result = result - conv_at(k, b, h) * factor
        start = b * WIDE + h * LANES
        coadd_ref[0, :, start : start + LANES] = result
    for index, e, t in others():
        stat_copy(index, me, tile, e, t).wait_send()


def window(sizes, template, science, plan, orders, coadd_weight, intersection):
    expos, tiles = (sizes["expo"], sizes["tile"])
    rows, width = template.shape[1:]
    cols = width // expos
    fits = (
        science.shape[1] == 1
        and template.shape[0] == 1
        and expos > 1
        and tiles > 1
        and width % expos == 0
        and cols % WIDE == 0
        and rows % 16 == 0
        and 3 * len(PAIRS) + 2 * NB + NU * expos <= LANES
    )
    if not fits:
        return per_device(template, science, plan, orders, coadd_weight, intersection)
    span = cols + 4 * LANES
    spare = 10368 * 1024
    dims = (expos, tiles, rows, width, cols)
    dma = pltpu.SemaphoreType.DMA
    scalar = pl.BlockSpec(memory_space=pltpu.SMEM)
    far = pl.BlockSpec(memory_space=pltpu.HBM)
    vector = pl.BlockSpec(memory_space=pltpu.VMEM)
    return pl.pallas_call(
        functools.partial(fused, dims),
        out_shape=(
            jax.ShapeDtypeStruct((1, rows, cols), jnp.float32),
            jax.ShapeDtypeStruct((1, 1, NU), jnp.float32),
        ),
        in_specs=[far, far, scalar, scalar, vector, vector],
        out_specs=(vector, vector),
        scratch_shapes=[
            pltpu.VMEM((expos, 3, rows, span), jnp.bfloat16),
            pltpu.VMEM((expos, rows, cols), jnp.bfloat16),
            pltpu.VMEM((expos, tiles, 1, 2 * LANES), jnp.float32),
            pltpu.VMEM((NB * rows, 3 * rows), jnp.bfloat16),
            pltpu.VMEM((NB, WIDE + 2 * LANES, WIDE), jnp.bfloat16),
            pltpu.VMEM((NB, rows * (cols // WIDE), WIDE), jnp.float32),
            pltpu.VMEM((LANES, LANES), jnp.float32),
            dma((2,)),
            dma((expos,)),
            dma((expos,)),
            dma((expos,)),
            dma((expos,)),
            dma((2, expos)),
            dma((2, expos)),
            dma((expos * tiles,)),
            dma((expos * tiles,)),
        ],
        compiler_params=pltpu.CompilerParams(collective_id=0, has_side_effects=True, vmem_limit_bytes=VMEM_BYTES - spare),
    )(template, science, plan, orders.T, coadd_weight, intersection)


def solution(mesh):
    return jax.shard_map(
        functools.partial(window, dict(mesh.shape)),
        mesh=mesh,
        in_specs=(
            P(("groups", "expo"), "tile", None),
            P(("groups", "expo"), None, "tile", None),
            P("groups"),
            P(),
            P(("groups", "expo"), None),
            P(("groups", "expo"), None),
        ),
        out_specs=(P("groups", "tile", "expo"), P(("groups", "expo"), None, None)),
        check_vma=False,
    )
```

```python
import functools

import jax
import jax.numpy as jnp
from jax import lax
from jax.experimental import pallas as pl
from jax.experimental.pallas import tpu as pltpu
from jax.sharding import PartitionSpec as P

HALF = 15
NB = 6
NU = 13


SIGMAS = (0.8, 1.4, 2.2, 3.0, 4.0, 5.5)
RIDGE = 0.05


def broadcast(block, axis, holder):
    block = jnp.where(lax.axis_index(axis) == holder, block, jnp.zeros_like(block))
    return lax.psum(block, axis)


def extended(x, sides, width):
    for axis, dim in sides:
        size, length = (lax.axis_size(axis), x.shape[dim])
        up = [(i, (i + 1) % size) for i in range(size - 1)]
        down = [(j, i) for i, j in up]
        last = lax.slice_in_dim(x, length - width, length, axis=dim)
        first = lax.slice_in_dim(x, 0, width, axis=dim)
        before = lax.ppermute(last, axis, up)
        after = lax.ppermute(first, axis, down)
        x = jnp.concatenate([before, x, after], axis=dim)
    return x


def make_filters(orders):
    taps_pos = jnp.arange(2 * HALF + 1).astype(jnp.float32) - HALF
    row_list = []
    col_list = []
    for basis in range(NB):
        sigma = SIGMAS[basis]
        envelope = jnp.exp(-taps_pos * taps_pos / (2.0 * sigma * sigma))

        def power(order):
            return jnp.where(order == 0, 1.0, jnp.where(order == 1, taps_pos, taps_pos * taps_pos))

        row_filter = envelope * power(orders[basis, 0])
        col_filter = envelope * power(orders[basis, 1])
        row_list.append(row_filter / jnp.sqrt(jnp.sum(row_filter * row_filter)))
        col_list.append(col_filter / jnp.sqrt(jnp.sum(col_filter * col_filter)))
    return (jnp.stack(row_list).astype(jnp.bfloat16), jnp.stack(col_list).astype(jnp.bfloat16))


def band_matrix(filters, out_len, in_len):
    offset = jnp.arange(in_len)[None, :] - jnp.arange(out_len)[:, None]
    taps_idx = jnp.arange(2 * HALF + 1)
    picks = (offset[:, :, None] == taps_idx[None, None, :]).astype(jnp.float32)
    band = jnp.einsum("ijt,kt->kij", picks, filters.astype(jnp.float32))
    return band.astype(jnp.bfloat16)


def per_device(template, science, plan, orders, coadd_weight, intersection):
    row_filters, col_filters = make_filters(orders)
    rows = template.shape[1]
    width = template.shape[2]
    blocks_count = width // 128
    steps_count = science.shape[1]
    row_band = band_matrix(row_filters, rows, rows + 2 * HALF)
    col_band = jnp.transpose(band_matrix(col_filters, 128, 128 + 2 * HALF), (0, 2, 1))
    column_pos = 2.0 * (jnp.arange(width).astype(jnp.float32) + 0.5) / width - 1.0
    pieces = []
    fitted = []
    for step in range(steps_count):
        owner_index = plan[step]
        received = broadcast(template[0], "expo", owner_index)
        padded = extended(received, (("tile", 0),), HALF)
        rowconv = jnp.einsum(
            "kij,jw->kiw", row_band, padded, preferred_element_type=jnp.float32
        ).astype(jnp.bfloat16)
        blocks = rowconv.reshape(NB, rows, blocks_count, 128)
        empty_rim = jnp.zeros((NB, rows, 1, HALF), jnp.bfloat16)
        previous = jnp.concatenate([empty_rim, blocks[:, :, :-1, 128 - HALF :]], axis=2)
        following = jnp.concatenate([blocks[:, :, 1:, :HALF], empty_rim], axis=2)
        window = jnp.concatenate([previous, blocks, following], axis=3)
        conv = jnp.einsum("krbj,kjc->krbc", window, col_band, preferred_element_type=jnp.float32)
        conv = conv.reshape(NB, rows, width)
        fields = jnp.concatenate(
            [conv, conv * column_pos, jnp.ones((1, rows, width), jnp.float32)], axis=0
        )
        fields = fields.reshape(NU, rows * width)
        exposure_image = science[0, step].astype(jnp.float32).reshape(rows * width)
        normal_local = jnp.dot(fields, fields.T, precision=lax.Precision.HIGHEST)
        project_local = jnp.dot(fields, exposure_image, precision=lax.Precision.HIGHEST)
        normal_matrix, projections = lax.psum((normal_local, project_local), "tile")
        normal_matrix = normal_matrix + RIDGE * (jnp.trace(normal_matrix) / NU) * jnp.eye(
            NU, dtype=jnp.float32
        )
        factor = jnp.linalg.cholesky(normal_matrix)
        coeffs = jax.scipy.linalg.cho_solve((factor, True), projections)
        model = jnp.dot(coeffs, fields, precision=lax.Precision.HIGHEST)
        difference = exposure_image - model
        weight_now = coadd_weight[0, step] * intersection[0, step].astype(jnp.float32)
        pieces.append((weight_now * difference).reshape(rows, width))
        fitted.append(coeffs)
    weighted = jnp.stack(pieces)
    received_parts = lax.all_to_all(weighted[None], "expo", split_axis=3, concat_axis=0, tiled=True)
    coadd = jnp.sum(received_parts, axis=0)
    return (coadd, jnp.stack(fitted)[None])


LANES = 128
VMEM_BYTES = 67043328
WIDE = 256
PAIRS = [(u, v) for u in range(NB) for v in range(u + 1)]
MESH = pl.DeviceIdType.MESH


def taps(position, sigma, order):
    power = jnp.where(order == 0, 1.0, jnp.where(order == 1, position, position * position))
    value = jnp.exp(-position * position / (2.0 * sigma * sigma)) * power
    return jnp.where(jnp.abs(position) <= HALF, value, 0.0)


def fused(
    dims,
    template_ref,
    science_ref,
    plan_ref,
    orders_ref,
    weight_ref,
    inter_ref,
    coadd_ref,
    coeffs_ref,
    tbuf,
    sbuf,
    rbuf,
    row_band,
    col_band,
    conv_ref,
    stat_ref,
    local_sem,
    tsend,
    trecv,
    ssend,
    srecv,
    fsend,
    frecv,
    rsend,
    rrecv,
):
    expos, tiles, rows, width, cols = dims
    per = cols // LANES
    span = cols + 2 * LANES
    blocks = cols // WIDE
    chunks = [(b, h) for b in range(blocks) for h in range(WIDE // LANES)]
    me = lax.axis_index("expo")
    tile = lax.axis_index("tile")

    def others():
        for de in range(expos):
            for dt in range(tiles):
                if de or dt:
                    yield de * tiles + dt, (me + de) % expos, (tile + dt) % tiles

    barrier = pltpu.get_barrier_semaphore()
    for d in range(1, expos):
        peer = (me + d) % expos
        pl.semaphore_signal(barrier, inc=1, device_id={"expo": peer}, device_id_type=MESH)
    for d in (1, tiles - 1):
        peer = (tile + d) % tiles
        pl.semaphore_signal(barrier, inc=1, device_id={"tile": peer}, device_id_type=MESH)

    def source_start(e):
        return e * per - 1 + (expos - 1 - e) // (expos - 1) - e // (expos - 1)

    def source_columns(e):
        return pl.ds(pl.multiple_of(source_start(e) * LANES, LANES), span)

    def window_columns(e):
        return pl.ds(pl.multiple_of((source_start(e) - e * per + 2) * LANES, LANES), span)

    def own_columns(e):
        return pl.ds(pl.multiple_of(e * cols, LANES), cols)

    mine = pltpu.make_async_copy(
        template_ref.at[0, :, source_columns(me)],
        tbuf.at[me, 1, :, window_columns(me)],
        local_sem.at[0],
    )
    mine.start()
    mine_science = pltpu.make_async_copy(
        science_ref.at[0, 0, :, own_columns(me)], sbuf.at[me], local_sem.at[1]
    )
    mine_science.start()

    def template_copy(d, target, holder):
        return pltpu.make_async_remote_copy(
            src_ref=template_ref.at[0, :, source_columns(target)],
            dst_ref=tbuf.at[holder, 1, :, window_columns(target)],
            send_sem=tsend.at[d],
            recv_sem=trecv.at[d],
            device_id={"expo": target},
            device_id_type=MESH,
        )

    def science_copy(d, target, holder):
        return pltpu.make_async_remote_copy(
            src_ref=science_ref.at[0, 0, :, own_columns(target)],
            dst_ref=sbuf.at[holder],
            send_sem=ssend.at[d],
            recv_sem=srecv.at[d],
            device_id={"expo": target},
            device_id_type=MESH,
        )

    def forward_copy(d, holder, side):
        target = tile + 1 if side == 0 else tile - 1
        return pltpu.make_async_remote_copy(
            src_ref=tbuf.at[holder, 1, :, window_columns(me)],
            dst_ref=tbuf.at[holder, 2 * side, :, window_columns(me)],
            send_sem=fsend.at[side, d],
            recv_sem=frecv.at[side, d],
            device_id={"tile": target},
            device_id_type=MESH,
        )

    def forward(d, holder):
        @pl.when(tile < tiles - 1)
        def _():
            forward_copy(d, holder, 0).start()

        @pl.when(tile > 0)
        def _():
            forward_copy(d, holder, 1).start()

    position = lax.broadcasted_iota(jnp.int32, (1, LANES), 1).astype(jnp.float32) - HALF
    for k in range(NB):
        sigma = SIGMAS[k]
        for side, length in ((0, rows), (1, LANES)):
            order = jnp.full((1, LANES), orders_ref[side, k], jnp.int32)
            line = taps(position, sigma, order)
            root = jnp.sqrt(jnp.sum(line * line, axis=1, keepdims=True))
            scale = 1.0 / root
            if side == 0:
                shape = (rows, 3 * rows)
                offset = (
                    lax.broadcasted_iota(jnp.int32, shape, 1)
                    - lax.broadcasted_iota(jnp.int32, shape, 0)
                    - rows
                ).astype(jnp.float32)
                band = taps(offset, sigma, jnp.full(shape, orders_ref[side, k], jnp.int32))
                row_band[k * rows : (k + 1) * rows, :] = (band * scale).astype(jnp.bfloat16)
            else:
                shape = (LANES, LANES)
                delta = lax.broadcasted_iota(jnp.int32, shape, 0) - lax.broadcasted_iota(
                    jnp.int32, shape, 1
                )
                column_order = jnp.full(shape, orders_ref[side, k], jnp.int32)
                zero = jnp.zeros(shape, jnp.bfloat16)
                parts = {}
                for kind in range(3):
                    offset = (delta + (kind - 1) * LANES).astype(jnp.float32)
                    band = taps(offset, sigma, column_order)
                    parts[kind] = (band * scale).astype(jnp.bfloat16)
                for jb in range(WIDE // LANES + 2):
                    for cb in range(WIDE // LANES):
                        col_band[
                            k,
                            jb * LANES : (jb + 1) * LANES,
                            cb * LANES : (cb + 1) * LANES,
                        ] = parts.get(jb - cb, zero)

    pl.semaphore_wait(barrier, expos + 1)
    for d in reversed(range(1, expos)):
        template_copy(d, (me + d) % expos, me).start()
    mine.wait()
    forward(0, me)
    for d in range(1, expos):
        science_copy(d, (me + d) % expos, me).start()

    for d in reversed(range(1, expos)):
        holder = (me + expos - d) % expos
        template_copy(d, me, holder).wait_recv()
        forward(d, holder)

    @pl.when(tile > 0)
    def _():
        for d in range(expos):
            forward_copy(d, (me + expos - d) % expos, 0).wait_recv()

    @pl.when(tile < tiles - 1)
    def _():
        for d in range(expos):
            forward_copy(d, (me + expos - d) % expos, 1).wait_recv()

    @pl.when(tile < tiles - 1)
    def _():
        for d in range(expos):
            forward_copy(d, (me + expos - d) % expos, 0).wait_send()

    @pl.when(tile > 0)
    def _():
        for d in range(expos):
            forward_copy(d, (me + expos - d) % expos, 1).wait_send()

    owner = plan_ref[0]
    shape = (rows, span)
    column = lax.broadcasted_iota(jnp.int32, shape, 1) + (me * cols - LANES)
    inside = (column >= 0) & (column < width)
    pieces = []
    for part in range(3):
        block = tbuf[owner, part, :, LANES : LANES + span].astype(jnp.float32)
        keep = inside
        if part == 0:
            keep = keep & (jnp.full(shape, tile, jnp.int32) > 0)
        if part == 2:
            keep = keep & (jnp.full(shape, tile, jnp.int32) < tiles - 1)
        pieces.append(jnp.where(keep, block, 0.0).astype(jnp.bfloat16))
    rows_window = jnp.concatenate(pieces, axis=0)
    rowconv = jnp.dot(
        row_band[...], rows_window, preferred_element_type=jnp.float32
    ).astype(jnp.bfloat16)
    for k in range(NB):
        mine_rows = rowconv[k * rows : (k + 1) * rows]
        windows = jnp.concatenate(
            [mine_rows[:, b * WIDE : (b + 1) * WIDE + 2 * LANES] for b in range(blocks)], axis=0
        )
        conv_ref[k] = jnp.dot(windows, col_band[k], preferred_element_type=jnp.float32)

    def conv_at(k, b, h):
        return conv_ref[k, b * rows : (b + 1) * rows, h * LANES : (h + 1) * LANES]

    def science_at(e, b, h):
        start = b * WIDE + h * LANES
        return sbuf[e, :, start : start + LANES].astype(jnp.float32)

    def fold(x):
        return x.reshape(rows // 8, 8, LANES).sum(axis=0)

    lane = lax.broadcasted_iota(jnp.int32, (1, LANES), 1)
    columns = {}
    for b, h in chunks:
        place = (me * cols + b * WIDE + h * LANES + lane).astype(jnp.float32)
        columns[b, h] = 2.0 * (place + 0.5) / width - 1.0

    def put(index, value):
        stat_ref[index : index + 1, :] = jnp.sum(value, axis=0, keepdims=True)

    count = 3 * len(PAIRS) + 2 * NB
    for index, (u, v) in enumerate(PAIRS):
        sums = [0.0, 0.0, 0.0]
        for b, h in chunks:
            product = fold(conv_at(u, b, h) * conv_at(v, b, h))
            once = product * columns[b, h]
            sums = [sums[0] + product, sums[1] + once, sums[2] + once * columns[b, h]]
        for moment in range(3):
            put(3 * index + moment, sums[moment])
    for u in range(NB):
        sums = [0.0, 0.0]
        for b, h in chunks:
            product = fold(conv_at(u, b, h))
            sums = [sums[0] + product, sums[1] + product * columns[b, h]]
        for moment in range(2):
            put(3 * len(PAIRS) + NB * moment + u, sums[moment])

    mine_science.wait()
    for d in range(1, expos):
        science_copy(d, me, (me + expos - d) % expos).wait_recv()
    for e in range(expos):
        for u in range(NB):
            sums = [0.0, 0.0]
            for b, h in chunks:
                product = fold(conv_at(u, b, h) * science_at(e, b, h))
                sums = [sums[0] + product, sums[1] + product * columns[b, h]]
            for moment in range(2):
                put(count + (NB * moment + u) * expos + e, sums[moment])
        total = 0.0
        for b, h in chunks:
            total = total + fold(science_at(e, b, h))
        put(count + 2 * NB * expos + e, total)
    used = count + NU * expos
    if used < LANES:
        stat_ref[used:LANES, :] = jnp.zeros((LANES - used, LANES), jnp.float32)

    reduced = jnp.sum(jnp.transpose(stat_ref[...]), axis=0, keepdims=True)
    weight = weight_ref[...] * inter_ref[...].astype(jnp.float32)
    rbuf[me, tile, :, :LANES] = reduced
    rbuf[me, tile, :, LANES:] = jnp.broadcast_to(weight, (1, LANES))

    def stat_copy(index, e, t, to_e, to_t):
        return pltpu.make_async_remote_copy(
            src_ref=rbuf.at[e, t],
            dst_ref=rbuf.at[e, t],
            send_sem=rsend.at[index],
            recv_sem=rrecv.at[index],
            device_id={"expo": to_e, "tile": to_t},
            device_id_type=MESH,
        )

    for index, e, t in others():
        stat_copy(index, me, tile, e, t).start()
    for d in range(1, expos):
        template_copy(d, (me + d) % expos, me).wait_send()
        science_copy(d, (me + d) % expos, me).wait_send()
    for de in range(expos):
        for dt in range(tiles):
            if de or dt:
                e = (me + expos - de) % expos
                t = (tile + tiles - dt) % tiles
                stat_copy(de * tiles + dt, e, t, e, t).wait_recv()

    total = rbuf[0, 0, :, :LANES]
    for e in range(expos):
        for t in range(tiles):
            if e or t:
                total = total + rbuf[e, t, :, :LANES]
    stat_ref[...] = jnp.transpose(jnp.broadcast_to(total, (LANES, LANES)))

    def value(index):
        return jnp.broadcast_to(stat_ref[index : index + 1, :], (expos, LANES))

    matrix = [[None] * NU for _ in range(NU)]
    for index, (u, v) in enumerate(PAIRS):
        plain, once, twice = (value(3 * index + moment) for moment in range(3))
        matrix[u][v] = plain
        matrix[NB + u][v] = once
        matrix[NB + v][u] = once
        matrix[NB + u][NB + v] = twice
    for u in range(2 * NB):
        matrix[2 * NB][u] = value(3 * len(PAIRS) + u)
    pixels = float(rows * tiles * width)
    matrix[2 * NB][2 * NB] = jnp.full((expos, LANES), pixels, jnp.float32)
    trace = matrix[0][0]
    for u in range(1, NU):
        trace = trace + matrix[u][u]
    ridge = RIDGE * (trace / NU)
    for u in range(NU):
        matrix[u][u] = matrix[u][u] + ridge
    right = [stat_ref[count + u * expos : count + (u + 1) * expos, :] for u in range(NU)]
    inverse = [None] * NU
    for j in range(NU):
        inverse[j] = 1.0 / matrix[j][j]
        for i in range(j + 1, NU):
            ratio = matrix[i][j] * inverse[j]
            for m in range(j + 1, i + 1):
                matrix[i][m] = matrix[i][m] - ratio * matrix[m][j]
            right[i] = right[i] - ratio * right[j]
    fitted = [None] * NU
    for j in reversed(range(NU)):
        left = right[j]
        for i in range(j + 1, NU):
            left = left - matrix[i][j] * fitted[i]
        fitted[j] = left * inverse[j]

    spread = lax.broadcasted_iota(jnp.int32, (expos, LANES), 1)
    table = jnp.zeros((expos, LANES), jnp.float32)
    for u in range(NU):
        table = jnp.where(spread == u, fitted[u], table)
    exposure = lax.broadcasted_iota(jnp.int32, (expos, LANES), 0)
    line = jnp.sum(jnp.where(exposure == me, table, 0.0), axis=0, keepdims=True)
    coeffs_ref[0] = line[:, :NU]

    weights = [rbuf[e, tile, :, LANES:] for e in range(expos)]
    stacked = jnp.concatenate(weights, axis=0)
    joint = [jnp.sum(stacked * fitted[u], axis=0, keepdims=True) for u in range(NU)]
    for b, h in chunks:
        result = science_at(0, b, h) * weights[0]
        for e in range(1, expos):
            result = result + science_at(e, b, h) * weights[e]
        result = result - joint[2 * NB]
        for k in range(NB):
            factor = joint[k] + columns[b, h] * joint[NB + k]
            result = result - conv_at(k, b, h) * factor
        start = b * WIDE + h * LANES
        coadd_ref[0, :, start : start + LANES] = result
    for index, e, t in others():
        stat_copy(index, me, tile, e, t).wait_send()


def window(sizes, template, science, plan, orders, coadd_weight, intersection):
    expos, tiles = (sizes["expo"], sizes["tile"])
    rows, width = template.shape[1:]
    cols = width // expos
    fits = (
        science.shape[1] == 1
        and template.shape[0] == 1
        and expos > 1
        and tiles > 1
        and width % expos == 0
        and cols % WIDE == 0
        and rows % 16 == 0
        and 3 * len(PAIRS) + 2 * NB + NU * expos <= LANES
    )
    if not fits:
        return per_device(template, science, plan, orders, coadd_weight, intersection)
    span = cols + 4 * LANES
    spare = 10368 * 1024
    dims = (expos, tiles, rows, width, cols)
    dma = pltpu.SemaphoreType.DMA
    scalar = pl.BlockSpec(memory_space=pltpu.SMEM)
    far = pl.BlockSpec(memory_space=pltpu.HBM)
    vector = pl.BlockSpec(memory_space=pltpu.VMEM)
    return pl.pallas_call(
        functools.partial(fused, dims),
        out_shape=(
            jax.ShapeDtypeStruct((1, rows, cols), jnp.float32),
            jax.ShapeDtypeStruct((1, 1, NU), jnp.float32),
        ),
        in_specs=[far, far, scalar, scalar, vector, vector],
        out_specs=(vector, vector),
        scratch_shapes=[
            pltpu.VMEM((expos, 3, rows, span), jnp.bfloat16),
            pltpu.VMEM((expos, rows, cols), jnp.bfloat16),
            pltpu.VMEM((expos, tiles, 1, 2 * LANES), jnp.float32),
            pltpu.VMEM((NB * rows, 3 * rows), jnp.bfloat16),
            pltpu.VMEM((NB, WIDE + 2 * LANES, WIDE), jnp.bfloat16),
            pltpu.VMEM((NB, rows * (cols // WIDE), WIDE), jnp.float32),
            pltpu.VMEM((LANES, LANES), jnp.float32),
            dma((2,)),
            dma((expos,)),
            dma((expos,)),
            dma((expos,)),
            dma((expos,)),
            dma((2, expos)),
            dma((2, expos)),
            dma((expos * tiles,)),
            dma((expos * tiles,)),
        ],
        compiler_params=pltpu.CompilerParams(collective_id=0, has_side_effects=True, vmem_limit_bytes=VMEM_BYTES - spare),
    )(template, science, plan, orders.T, coadd_weight, intersection)


def solution(mesh):
    return jax.shard_map(
        functools.partial(window, dict(mesh.shape)),
        mesh=mesh,
        in_specs=(
            P(("groups", "expo"), "tile", None),
            P(("groups", "expo"), None, "tile", None),
            P("groups"),
            P(),
            P(("groups", "expo"), None),
            P(("groups", "expo"), None),
        ),
        out_specs=(P("groups", "tile", "expo"), P(("groups", "expo"), None, None)),
        check_vma=False,
    )
```
